32 devices in a mesh: island: 2 (over x), fsdp: 16 (over z, y, core).
Axes of the slice: x: 2, y: 2, z: 4, core: 2. Of those that a mesh axis runs over, the one named last changes fastest.
Arguments:
- inputs: bfloat16 [4096, 4096], P(('island', 'fsdp')), may hold values from -6 to 6
- key_grad: bfloat16 [4096, 512], P(('island', 'fsdp')), may hold values from -6 to 6
- weight: float32 [4096, 512], P('fsdp'), may hold values from -6 to 6
- gain: float32 [4096], P('fsdp'), may hold values from 0.25 to 1.75
- momentum: float32 [4096, 512], P('fsdp'), may hold values from -3 to 3
- gain_momentum: float32 [4096], P('fsdp'), may hold values from -3 to 3
Outputs:
- keys: bfloat16 [4096, 512], P(('island', 'fsdp'))
- input_gradient: bfloat16 [4096, 4096], P(('island', 'fsdp'))
- new_weight: float32 [4096, 512], P('fsdp')
- new_momentum: float32 [4096, 512], P('fsdp')
- new_gain: float32 [4096], P('fsdp')
- new_gain_momentum: float32 [4096], P('fsdp')
The draws below stay inside these ranges and needn't reach their ends.
All inputs are finite; a program needn't handle non-finite values.
Results may differ from the reference program's by a relative error of at most 0.009.
Values may be sent and summed in bfloat16 or wider, within the bound.
A program may use at most 64 MiB of HBM per device.

```python
import jax
import jax.numpy as jnp
from jax import lax

D = 4096
C = 512
TOKENS = 4096
N_ISLAND = 2


def block_scale(key, dims, split, least, top_value):
    level, own = 1.0, jax.random.fold_in(key, 6)
    for dim, blocks in split:
        steps = jnp.exp(jax.random.uniform(jax.random.fold_in(own, dim), (blocks,), jnp.float32, least / len(split), top_value / len(split)))
        level = level * jnp.repeat(steps, dims[dim] // blocks).reshape([-1 if axis == dim else 1 for axis in range(len(dims))])
    return level


def normal_values(own_key, dims, deviation, reach, split=(), held_as=jnp.bfloat16):
    level = block_scale(own_key, dims, split, -0.22, 0.18) if split else 1.0
    values = jax.random.normal(own_key, dims, jnp.float32) * deviation * level
    return jnp.minimum(jnp.maximum(values, -reach), reach).astype(held_as)


def setup_inputs(seed: int = 0) -> dict:
    splits = jax.random.split(jax.random.key(seed), 7)
    return {
        "inputs": normal_values(splits[0], (TOKENS, D), 1.0, 6.0, ((0, 32),)),
        "key_grad": normal_values(splits[1], (TOKENS, C), 1.0, 6.0, ((0, 32),)),
        "weight": normal_values(splits[2], (D, C), 1.0, 6.0, ((0, 16),), jnp.float32),
        "gain": jnp.clip(1.0 + 0.15 * jax.random.normal(splits[3], (D,), jnp.float32), 0.25, 1.75),
        "momentum": normal_values(splits[4], (D, C), 0.5, 3.0, ((0, 16),), jnp.float32),
        "gain_momentum": normal_values(splits[5], (D,), 0.5, 3.0, ((0, 16),), jnp.float32),
    }


epsilon = 1e-05
inner_rate = 0.5
gain_rate = 0.02
beta_momentum = 0.9
outer_rate = 0.7

def island_pass(operands, weight_b, gain_broadcast):
    acts, cotangent = operands
    scale = D ** (-0.5)
    expanded_rows = acts.astype(jnp.float32)
    inverse_norm = lax.rsqrt(lax.optimization_barrier(jnp.mean(expanded_rows * expanded_rows, axis=1, keepdims=True)) + epsilon)
    centered_input = expanded_rows * inverse_norm
    normalized_rows = (centered_input * gain_broadcast.astype(jnp.float32)).astype(jnp.bfloat16)
    keys = (jnp.dot(normalized_rows, weight_b, preferred_element_type=jnp.float32) * scale).astype(jnp.bfloat16)
    normalized_gradient = jnp.dot(cotangent, weight_b.T, preferred_element_type=jnp.float32) * scale
    gain_gradient = lax.optimization_barrier(jnp.sum(normalized_gradient * centered_input, axis=0))
    centered_gradient = normalized_gradient * gain_broadcast.astype(jnp.float32)
    key_output = lax.optimization_barrier(jnp.mean(centered_gradient * centered_input, axis=1, keepdims=True))
    input_gradient = (inverse_norm * (centered_gradient - centered_input * key_output)).astype(jnp.bfloat16)
    weight_grad = jnp.dot(normalized_rows.T, cotangent, preferred_element_type=jnp.float32) * scale
    return (keys, input_gradient, inner_rate * weight_grad, gain_rate * gain_gradient)

def reference(inputs, key_grad, weight, gain, momentum, gain_momentum):
    weight_b = weight.astype(jnp.bfloat16)
    gain_broadcast = gain.astype(jnp.bfloat16)
    island_tokens = inputs.shape[0] // N_ISLAND
    acts = inputs.reshape(N_ISLAND, island_tokens, inputs.shape[1])
    cotangents = key_grad.reshape(N_ISLAND, island_tokens, key_grad.shape[1])
    keys, input_gradient, weight_deltas, gain_deltas = lax.map(lambda ops: island_pass(ops, weight_b, gain_broadcast), (acts, cotangents))
    mean_delta = lax.optimization_barrier(jnp.sum(weight_deltas, axis=0)) / N_ISLAND
    gain_delta = lax.optimization_barrier(jnp.sum(gain_deltas, axis=0)) / N_ISLAND
    new_momentum = beta_momentum * momentum + mean_delta
    new_weight = weight - outer_rate * (mean_delta + beta_momentum * new_momentum)
    new_gain_momentum = beta_momentum * gain_momentum + gain_delta
    new_gain = gain - outer_rate * (gain_delta + beta_momentum * new_gain_momentum)
    keys = keys.reshape(inputs.shape[0], key_grad.shape[1])
    input_gradient = input_gradient.reshape(inputs.shape)
    return (keys, input_gradient, new_weight, new_momentum, new_gain, new_gain_momentum)
```

```python
import functools

import jax
import jax.numpy as jnp
from jax import lax
from jax.experimental import pallas as pl
from jax.experimental.pallas import tpu as pltpu
from jax.sharding import PartitionSpec as P

epsilon = 1e-05
inner_rate = 0.5
gain_rate = 0.02
beta_momentum = 0.9
outer_rate = 0.7

MESH = pl.DeviceIdType.MESH
F32, BF16 = jnp.float32, jnp.bfloat16


def kernel(
    n_isl, a, b,
    x_ref, kg_ref, w_ref, g_ref, m_ref, gm_ref,
    keys_ref, ig_ref, nw_ref, nm_ref, ng_ref, ngm_ref,
    gw, xs, xr, kr, gs, gr, ge, dx, kacc,
    z_s, z_r, y_s, y_r, x_s, x_r, c_s, c_r, t_s, t_r, k_s, k_r, g_s, g_r, e_s, e_r,
):
    nq = 2 * b
    n = a * nq
    tokens, width = x_ref.shape
    rows, feats = w_ref.shape
    scale = width ** (-0.5)
    isl = lax.axis_index("island")
    f = lax.axis_index("fsdp")
    z, q = f // nq, f % nq
    y, core = q // 2, q % 2
    sib = y * 2 + 1 - core
    half = isl % 2
    partner = isl + 1 - 2 * half

    def dev(i, zz, qq):
        return (i, zz * nq + qq)

    def remote(src, dst, ss, rs, to):
        return pltpu.make_async_remote_copy(
            src_ref=src, dst_ref=dst, send_sem=ss, recv_sem=rs, device_id=to, device_id_type=MESH
        )

    zs_ = [lax.rem(z + k, a) for k in range(a)]
    qs_ = [lax.rem(q + k, nq) for k in range(nq)]
    ys_ = [lax.rem(y + k, b) for k in range(b)]
    is_ = [lax.rem(isl + k, n_isl) for k in range(n_isl)]

    barrier = pltpu.get_barrier_semaphore()
    for k in range(1, a):
        pl.semaphore_signal(barrier, inc=1, device_id=dev(isl, zs_[k], q), device_id_type=MESH)
    for k in range(1, nq):
        pl.semaphore_signal(barrier, inc=1, device_id=dev(isl, z, qs_[k]), device_id_type=MESH)
    for k in range(1, n_isl):
        pl.semaphore_signal(barrier, inc=1, device_id=dev(is_[k], z, q), device_id_type=MESH)

    lanes = min(rows, 128)
    gain_col = jnp.concatenate(
        [
            jnp.broadcast_to(
                g_ref[0:1, j * lanes : (j + 1) * lanes].astype(BF16).astype(F32), (lanes, lanes)
            ).T[:, 0:1]
            for j in range(rows // lanes)
        ],
        axis=0,
    )
    w_b = w_ref[...].astype(BF16).astype(F32)
    gw[z, q] = (w_b * gain_col).astype(BF16).reshape(2, rows // 2, feats)
    pl.semaphore_wait(barrier, a - 1 + nq - 1 + n_isl - 1)

    sends = []

    def go(copy):
        copy.start()
        sends.append(copy)

    def z_copy(k):
        p = gw.at[z, q, half]
        return remote(p, p, z_s.at[k], z_r.at[k], dev(isl, zs_[k], q))

    def z_wait(k):
        p = gw.at[lax.rem(z + a - k, a), q, half]
        remote(p, p, z_s.at[k], z_r.at[k], dev(isl, zs_[k], q)).wait_recv()

    def y_copy(zk, k):
        p = gw.at[lax.rem(z + a - zk, a), q, half]
        return remote(p, p, y_s.at[zk, k], y_r.at[zk, k], dev(isl, z, ys_[k] * 2 + core))

    def y_wait(zk, k):
        p = gw.at[lax.rem(z + a - zk, a), lax.rem(y + b - k, b) * 2 + core, half]
        remote(p, p, y_s.at[zk, k], y_r.at[zk, k], dev(isl, z, q)).wait_recv()

    def piece(zk, k):
        return lax.rem(z + a - zk, a), lax.rem(y + b - k, b) * 2 + core

    def x_copy(zk, k):
        zz, qq = piece(zk, k)
        p = gw.at[zz, qq, half]
        return remote(p, p, x_s.at[zk, k], x_r.at[zk, k], dev(partner, z, q))

    def x_wait(zk, k):
        zz, qq = piece(zk, k)
        p = gw.at[zz, qq, 1 - half]
        remote(p, p, x_s.at[zk, k], x_r.at[zk, k], dev(partner, z, q)).wait_recv()

    def c_copy(zk, k, h):
        zz, qq = piece(zk, k)
        p = gw.at[zz, qq, lax.rem(half + h, 2)]
        return remote(p, p, c_s.at[zk, k, h], c_r.at[zk, k, h], dev(isl, z, sib))

    def c_wait(zk, k, h):
        zz, qq = piece(zk, k)
        p = gw.at[zz, qq + 1 - 2 * core, lax.rem(half + h, 2)]
        remote(p, p, c_s.at[zk, k, h], c_r.at[zk, k, h], dev(isl, z, sib)).wait_recv()

    for k in range(1, a):
        go(z_copy(k))

    for k in range(1, nq):
        go(remote(kg_ref, kr.at[q], k_s.at[k], k_r.at[k], dev(isl, z, qs_[k])))

    acc = jnp.zeros((tokens, rows), F32)
    for p in range(n):
        xc = x_ref[:, p * rows : (p + 1) * rows].astype(F32)
        acc = acc + xc * xc
    r = lax.rsqrt(jnp.sum(acc, axis=1, keepdims=True) * (1.0 / width) + epsilon)
    for p in range(n):
        xc = x_ref[:, p * rows : (p + 1) * rows].astype(F32)
        xs[p % nq, p // nq] = (xc * r).astype(BF16)
    for k in range(1, nq):
        go(remote(xs.at[qs_[k]], xr.at[q], t_s.at[k], t_r.at[k], dev(isl, z, qs_[k])))
    xr[q] = xs[q]
    kr[q] = kg_ref[...]

    for k in range(1, b):
        go(y_copy(0, k))
    for h in range(2):
        go(c_copy(0, 0, h))

    for zk in range(1, a):
        z_wait(zk)
        for k in range(1, b):
            go(y_copy(zk, k))
        go(x_copy(zk, 0))
        go(c_copy(zk, 0, 0))

    for k in range(1, nq):
        src = lax.rem(q + nq - k, nq)
        remote(kg_ref, kr.at[src], k_s.at[k], k_r.at[k], dev(isl, z, q)).wait_recv()
        remote(xs.at[q], xr.at[src], t_s.at[k], t_r.at[k], dev(isl, z, q)).wait_recv()

    def partial(zz):
        return lax.dot_general(
            xr[:, zz].reshape(nq * tokens, rows),
            kr[...].reshape(nq * tokens, feats),
            (((0,), (0,)), ((), ())),
            preferred_element_type=F32,
        )

    for k in range(1, a):
        gs[k] = partial(zs_[k]).astype(BF16)
        go(remote(gs.at[k], gr.at[k], g_s.at[k], g_r.at[k], dev(isl, zs_[k], q)))
    own = partial(z)

    for zk in range(a):
        for k in range(1, b):
            y_wait(zk, k)
            go(x_copy(zk, k))
            go(c_copy(zk, k, 0))

    for k in range(1, a):
        remote(gs.at[k], gr.at[k], g_s.at[k], g_r.at[k], dev(isl, z, q)).wait_recv()
        own = own + gr[k].astype(F32)
    ge[isl] = own.astype(BF16)
    for k in range(1, n_isl):
        go(remote(ge.at[isl], ge.at[isl], e_s.at[k], e_r.at[k], dev(is_[k], z, q)))

    kacc[...] = jnp.zeros_like(kacc)

    def use(zz, qq):
        p = gw[zz, qq].reshape(rows, feats)
        kacc[...] += jnp.dot(xs[qq, zz], p, preferred_element_type=F32)
        dx[qq, zz] = lax.dot_general(
            kg_ref[...], p, (((1,), (1,)), ((), ())), preferred_element_type=F32
        )

    order = [(zk, k) for k in range(b) for zk in range(a)]
    for zk, k in order:
        if (zk, k) != (0, 0):
            x_wait(zk, k)
            go(c_copy(zk, k, 1))
        use(*piece(zk, k))
    for zk, k in order:
        c_wait(zk, k, 0)
        c_wait(zk, k, 1)
        zz, qq = piece(zk, k)
        use(zz, qq + 1 - 2 * core)

    keys_ref[...] = (kacc[...] * scale).astype(BF16)
    acc = jnp.zeros((tokens, rows), F32)
    for p in range(n):
        xh = x_ref[:, p * rows : (p + 1) * rows].astype(F32) * r
        acc = acc + dx[p % nq, p // nq] * xh
    mean = jnp.sum(acc, axis=1, keepdims=True) * (scale / width)
    for p in range(n):
        cols = slice(p * rows, (p + 1) * rows)
        xh = x_ref[:, cols].astype(F32) * r
        ig_ref[:, cols] = (r * (dx[p % nq, p // nq] * scale - xh * mean)).astype(BF16)

    for k in range(1, n_isl):
        src = lax.rem(isl + n_isl - k, n_isl)
        remote(ge.at[src], ge.at[src], e_s.at[k], e_r.at[k], dev(isl, z, q)).wait_recv()
    total = ge[0].astype(F32)
    for k in range(1, n_isl):
        total = total + ge[k].astype(F32)
    total = total * (scale / n_isl)
    delta = total * gain_col * inner_rate
    w = w_ref[...]
    fresh = beta_momentum * m_ref[...] + delta
    nm_ref[...] = fresh
    nw_ref[...] = w - outer_rate * (delta + beta_momentum * fresh)
    gain_sum = jnp.sum(w.astype(BF16).astype(F32) * total, axis=1, keepdims=True) * gain_rate
    for j in range(rows // lanes):
        s = slice(j * lanes, (j + 1) * lanes)
        d = jnp.broadcast_to(gain_sum[s], (lanes, lanes)).T[0:1]
        fresh = beta_momentum * gm_ref[0:1, s] + d
        ngm_ref[0:1, s] = fresh
        ng_ref[0:1, s] = g_ref[0:1, s] - outer_rate * (d + beta_momentum * fresh)

    for copy in sends:
        copy.wait_send()


def solution(mesh):
    n_isl, n = mesh.shape["island"], mesh.shape["fsdp"]
    b = 1
    while 4 * b * b <= n // 2:
        b *= 2
    a = n // 2 // b
    nq = 2 * b

    def shards(inputs, key_grad, weight, gain, momentum, gain_momentum):
        tokens, width = inputs.shape
        rows, feats = weight.shape
        sd = jax.ShapeDtypeStruct
        dma = pltpu.SemaphoreType.DMA
        vm = pl.BlockSpec(memory_space=pltpu.VMEM)
        outs = pl.pallas_call(
            functools.partial(kernel, n_isl, a, b),
            out_shape=(
                sd((tokens, feats), BF16),
                sd((tokens, width), BF16),
                sd((rows, feats), F32),
                sd((rows, feats), F32),
                sd((1, rows), F32),
                sd((1, rows), F32),
            ),
            in_specs=[vm] * 6,
            out_specs=[vm] * 6,
            scratch_shapes=[
                pltpu.VMEM((a, nq, 2, rows // 2, feats), BF16),
                pltpu.VMEM((nq, a, tokens, rows), BF16),
                pltpu.VMEM((nq, a, tokens, rows), BF16),
                pltpu.VMEM((nq, tokens, feats), BF16),
                pltpu.VMEM((a, rows, feats), BF16),
                pltpu.VMEM((a, rows, feats), BF16),
                pltpu.VMEM((n_isl, rows, feats), BF16),
                pltpu.VMEM((nq, a, tokens, rows), F32),
                pltpu.VMEM((tokens, feats), F32),
                dma((a,)), dma((a,)),
                dma((a, b)), dma((a, b)),
                dma((a, b)), dma((a, b)),
                dma((a, b, 2)), dma((a, b, 2)),
                dma((nq,)), dma((nq,)),
                dma((nq,)), dma((nq,)),
                dma((a,)), dma((a,)),
                dma((n_isl,)), dma((n_isl,)),
            ],
            compiler_params=pltpu.CompilerParams(
                collective_id=0, has_side_effects=True, vmem_limit_bytes=48 << 20
            ),
        )(inputs, key_grad, weight, gain.reshape(1, rows), momentum, gain_momentum.reshape(1, rows))
        keys, ig, nw, nm, ng, ngm = outs
        return keys, ig, nw, nm, ng.reshape(rows), ngm.reshape(rows)

    in_specs = (
        P(("island", "fsdp"), None),
        P(("island", "fsdp"), None),
        P("fsdp", None),
        P("fsdp"),
        P("fsdp", None),
        P("fsdp"),
    )
    out_specs = (
        P(("island", "fsdp"), None),
        P(("island", "fsdp"), None),
        P("fsdp", None),
        P("fsdp", None),
        P("fsdp"),
        P("fsdp"),
    )
    return jax.shard_map(shards, mesh=mesh, in_specs=in_specs, out_specs=out_specs, check_vma=False)
```

```python
import functools

import jax
import jax.numpy as jnp
from jax import lax
from jax.experimental import pallas as pl
from jax.experimental.pallas import tpu as pltpu
from jax.sharding import PartitionSpec as P

epsilon = 1e-05
inner_rate = 0.5
gain_rate = 0.02
beta_momentum = 0.9
outer_rate = 0.7

MESH = pl.DeviceIdType.MESH
F32, BF16 = jnp.float32, jnp.bfloat16


def kernel(
    n_isl, a, b,
    x_hbm, kg_hbm, w_hbm, g_ref, m_hbm, gm_ref,
    keys_ref, ig_ref, nw_ref, nm_ref, ng_ref, ngm_ref,
    x_ref, kg_ref, w_ref, m_ref, gw, xs, xr, kr, gs, gr, ge, dx, kacc, load,
    z_s, z_r, y_s, y_r, x_s, x_r, c_s, c_r, t_s, t_r, k_s, k_r, g_s, g_r, e_s, e_r,
):
    nq = 2 * b
    n = a * nq
    tokens, width = x_ref.shape
    rows, feats = w_ref.shape
    scale = width ** (-0.5)
    isl = lax.axis_index("island")
    f = lax.axis_index("fsdp")
    z, q = f // nq, f % nq
    y, core = q // 2, q % 2
    sib = y * 2 + 1 - core
    half = isl % 2
    partner = isl + 1 - 2 * half

    def dev(i, zz, qq):
        return (i, zz * nq + qq)

    def remote(src, dst, ss, rs, to):
        return pltpu.make_async_remote_copy(
            src_ref=src, dst_ref=dst, send_sem=ss, recv_sem=rs, device_id=to, device_id_type=MESH
        )

    zs_ = [lax.rem(z + k, a) for k in range(a)]
    qs_ = [lax.rem(q + k, nq) for k in range(nq)]
    ys_ = [lax.rem(y + k, b) for k in range(b)]
    is_ = [lax.rem(isl + k, n_isl) for k in range(n_isl)]

    loads = [
        pltpu.make_async_copy(src, dst, load.at[i])
        for i, (src, dst) in enumerate(
            ((w_hbm, w_ref), (kg_hbm, kg_ref), (x_hbm, x_ref), (m_hbm, m_ref))
        )
    ]
    for copy in loads:
        copy.start()
    barrier = pltpu.get_barrier_semaphore()
    for k in range(1, a):
        pl.semaphore_signal(barrier, inc=1, device_id=dev(isl, zs_[k], q), device_id_type=MESH)
    for k in range(1, nq):
        pl.semaphore_signal(barrier, inc=1, device_id=dev(isl, z, qs_[k]), device_id_type=MESH)
    for k in range(1, n_isl):
        pl.semaphore_signal(barrier, inc=1, device_id=dev(is_[k], z, q), device_id_type=MESH)

    lanes = min(rows, 128)
    gain_col = jnp.concatenate(
        [
            jnp.broadcast_to(
                g_ref[0:1, j * lanes : (j + 1) * lanes].astype(BF16).astype(F32), (lanes, lanes)
            ).T[:, 0:1]
            for j in range(rows // lanes)
        ],
        axis=0,
    )
    loads[0].wait()
    w_b = w_ref[...].astype(BF16).astype(F32)
    gw[z, q] = (w_b * gain_col).astype(BF16).reshape(2, rows // 2, feats)
    pl.semaphore_wait(barrier, a - 1 + nq - 1 + n_isl - 1)

    sends = []

    def go(copy):
        copy.start()
        sends.append(copy)

    def z_copy(k):
        p = gw.at[z, q, half]
        return remote(p, p, z_s.at[k], z_r.at[k], dev(isl, zs_[k], q))

    def z_wait(k):
        p = gw.at[lax.rem(z + a - k, a), q, half]
        remote(p, p, z_s.at[k], z_r.at[k], dev(isl, zs_[k], q)).wait_recv()

    def y_copy(zk, k):
        p = gw.at[lax.rem(z + a - zk, a), q, half]
        return remote(p, p, y_s.at[zk, k], y_r.at[zk, k], dev(isl, z, ys_[k] * 2 + core))

    def y_wait(zk, k):
        p = gw.at[lax.rem(z + a - zk, a), lax.rem(y + b - k, b) * 2 + core, half]
        remote(p, p, y_s.at[zk, k], y_r.at[zk, k], dev(isl, z, q)).wait_recv()

    def piece(zk, k):
        return lax.rem(z + a - zk, a), lax.rem(y + b - k, b) * 2 + core

    def x_copy(zk, k):
        zz, qq = piece(zk, k)
        p = gw.at[zz, qq, half]
        return remote(p, p, x_s.at[zk, k], x_r.at[zk, k], dev(partner, z, q))

    def x_wait(zk, k):
        zz, qq = piece(zk, k)
        p = gw.at[zz, qq, 1 - half]
        remote(p, p, x_s.at[zk, k], x_r.at[zk, k], dev(partner, z, q)).wait_recv()

    def c_copy(zk, k, h):
        zz, qq = piece(zk, k)
        p = gw.at[zz, qq, lax.rem(half + h, 2)]
        return remote(p, p, c_s.at[zk, k, h], c_r.at[zk, k, h], dev(isl, z, sib))

    def c_wait(zk, k, h):
        zz, qq = piece(zk, k)
        p = gw.at[zz, qq + 1 - 2 * core, lax.rem(half + h, 2)]
        remote(p, p, c_s.at[zk, k, h], c_r.at[zk, k, h], dev(isl, z, sib)).wait_recv()

    for k in range(1, a):
        go(z_copy(k))
    loads[1].wait()

    for k in range(1, nq):
        go(remote(kg_ref, kr.at[q], k_s.at[k], k_r.at[k], dev(isl, z, qs_[k])))

    loads[2].wait()
    acc = jnp.zeros((tokens, rows), F32)
    for p in range(n):
        xc = x_ref[:, p * rows : (p + 1) * rows].astype(F32)
        acc = acc + xc * xc
    r = lax.rsqrt(jnp.sum(acc, axis=1, keepdims=True) * (1.0 / width) + epsilon)
    for p in range(n):
        xc = x_ref[:, p * rows : (p + 1) * rows].astype(F32)
        xs[p % nq, p // nq] = (xc * r).astype(BF16)
    near = list(range(1, a)) + [0]
    for j in near:
        for k in range(1, nq):
            go(
                remote(
                    xs.at[qs_[k], zs_[j]], xr.at[q, zs_[j]],
                    t_s.at[j, k], t_r.at[j, k], dev(isl, z, qs_[k]),
                )
            )
    xr[q] = xs[q]
    kr[q] = kg_ref[...]

    for k in range(1, b):
        go(y_copy(0, k))
    for h in range(2):
        go(c_copy(0, 0, h))

    for zk in range(1, a):
        z_wait(zk)
        for k in range(1, b):
            go(y_copy(zk, k))
        go(x_copy(zk, 0))
        go(c_copy(zk, 0, 0))

    for k in range(1, nq):
        src = lax.rem(q + nq - k, nq)
        remote(kg_ref, kr.at[src], k_s.at[k], k_r.at[k], dev(isl, z, q)).wait_recv()

    def partial(j):
        zz = zs_[j]
        for k in range(1, nq):
            src = lax.rem(q + nq - k, nq)
            remote(
                xs.at[q, zz], xr.at[src, zz], t_s.at[j, k], t_r.at[j, k], dev(isl, z, q)
            ).wait_recv()
        return lax.dot_general(
            xr[:, zz].reshape(nq * tokens, rows),
            kr[...].reshape(nq * tokens, feats),
            (((0,), (0,)), ((), ())),
            preferred_element_type=F32,
        )

    for k in range(1, a):
        gs[k] = partial(k).astype(BF16)
        go(remote(gs.at[k], gr.at[k], g_s.at[k], g_r.at[k], dev(isl, zs_[k], q)))
    own = partial(0)

    for zk in range(a):
        for k in range(1, b):
            y_wait(zk, k)
            go(x_copy(zk, k))
            go(c_copy(zk, k, 0))

    for k in range(1, a):
        remote(gs.at[k], gr.at[k], g_s.at[k], g_r.at[k], dev(isl, z, q)).wait_recv()
        own = own + gr[k].astype(F32)
    ge[isl] = own.astype(BF16)
    for k in range(1, n_isl):
        go(remote(ge.at[isl], ge.at[isl], e_s.at[k], e_r.at[k], dev(is_[k], z, q)))

    kacc[...] = jnp.zeros_like(kacc)

    def use(zz, qq):
        p = gw[zz, qq].reshape(rows, feats)
        kacc[...] += jnp.dot(xs[qq, zz], p, preferred_element_type=F32)
        dx[qq, zz] = lax.dot_general(
            kg_ref[...], p, (((1,), (1,)), ((), ())), preferred_element_type=F32
        )

    order = [(zk, k) for k in range(b) for zk in range(a)]
    for zk, k in order:
        if (zk, k) != (0, 0):
            x_wait(zk, k)
            go(c_copy(zk, k, 1))
        use(*piece(zk, k))
    for zk, k in order:
        c_wait(zk, k, 0)
        c_wait(zk, k, 1)
        zz, qq = piece(zk, k)
        use(zz, qq + 1 - 2 * core)

    keys_ref[...] = (kacc[...] * scale).astype(BF16)
    acc = jnp.zeros((tokens, rows), F32)
    for p in range(n):
        xh = x_ref[:, p * rows : (p + 1) * rows].astype(F32) * r
        acc = acc + dx[p % nq, p // nq] * xh
    mean = jnp.sum(acc, axis=1, keepdims=True) * (scale / width)
    for p in range(n):
        cols = slice(p * rows, (p + 1) * rows)
        xh = x_ref[:, cols].astype(F32) * r
        ig_ref[:, cols] = (r * (dx[p % nq, p // nq] * scale - xh * mean)).astype(BF16)

    for k in range(1, n_isl):
        src = lax.rem(isl + n_isl - k, n_isl)
        remote(ge.at[src], ge.at[src], e_s.at[k], e_r.at[k], dev(isl, z, q)).wait_recv()
    total = ge[0].astype(F32)
    for k in range(1, n_isl):
        total = total + ge[k].astype(F32)
    total = total * (scale / n_isl)
    delta = total * gain_col * inner_rate
    w = w_ref[...]
    loads[3].wait()
    fresh = beta_momentum * m_ref[...] + delta
    nm_ref[...] = fresh
    nw_ref[...] = w - outer_rate * (delta + beta_momentum * fresh)
    gain_sum = jnp.sum(w.astype(BF16).astype(F32) * total, axis=1, keepdims=True) * gain_rate
    for j in range(rows // lanes):
        s = slice(j * lanes, (j + 1) * lanes)
        d = jnp.broadcast_to(gain_sum[s], (lanes, lanes)).T[0:1]
        fresh = beta_momentum * gm_ref[0:1, s] + d
        ngm_ref[0:1, s] = fresh
        ng_ref[0:1, s] = g_ref[0:1, s] - outer_rate * (d + beta_momentum * fresh)

    for copy in sends:
        copy.wait_send()


def store(*refs):
    k = (len(refs) - 1) // 2
    sem = refs[-1]
    copies = [pltpu.make_async_copy(refs[i], refs[k + i], sem.at[i]) for i in range(k)]
    for copy in copies:
        copy.start()
    for copy in copies:
        copy.wait()


def solution(mesh):
    n_isl, n = mesh.shape["island"], mesh.shape["fsdp"]
    b = 1
    while 4 * b * b <= n // 2:
        b *= 2
    a = n // 2 // b
    nq = 2 * b

    def shards(inputs, key_grad, weight, gain, momentum, gain_momentum):
        tokens, width = inputs.shape
        rows, feats = weight.shape
        sd = jax.ShapeDtypeStruct
        dma = pltpu.SemaphoreType.DMA
        vm = pl.BlockSpec(memory_space=pltpu.VMEM)
        hbm = pl.BlockSpec(memory_space=pltpu.HBM)
        shapes = (
            sd((tokens, feats), BF16),
            sd((tokens, width), BF16),
            sd((rows, feats), F32),
            sd((rows, feats), F32),
            sd((1, rows), F32),
            sd((1, rows), F32),
        )
        outs = pl.pallas_call(
            functools.partial(kernel, n_isl, a, b),
            out_shape=shapes,
            in_specs=[hbm, hbm, hbm, vm, hbm, vm],
            out_specs=[vm] * 6,
            scratch_shapes=[
                pltpu.VMEM((tokens, width), BF16),
                pltpu.VMEM((tokens, feats), BF16),
                pltpu.VMEM((rows, feats), F32),
                pltpu.VMEM((rows, feats), F32),
                pltpu.VMEM((a, nq, 2, rows // 2, feats), BF16),
                pltpu.VMEM((nq, a, tokens, rows), BF16),
                pltpu.VMEM((nq, a, tokens, rows), BF16),
                pltpu.VMEM((nq, tokens, feats), BF16),
                pltpu.VMEM((a, rows, feats), BF16),
                pltpu.VMEM((a, rows, feats), BF16),
                pltpu.VMEM((n_isl, rows, feats), BF16),
                pltpu.VMEM((nq, a, tokens, rows), F32),
                pltpu.VMEM((tokens, feats), F32),
                dma((4,)),
                dma((a,)), dma((a,)),
                dma((a, b)), dma((a, b)),
                dma((a, b)), dma((a, b)),
                dma((a, b, 2)), dma((a, b, 2)),
                dma((a, nq)), dma((a, nq)),
                dma((nq,)), dma((nq,)),
                dma((a,)), dma((a,)),
                dma((n_isl,)), dma((n_isl,)),
            ],
            compiler_params=pltpu.CompilerParams(
                collective_id=0, has_side_effects=True, vmem_limit_bytes=48 << 20
            ),
        )(inputs, key_grad, weight, gain.reshape(1, rows), momentum, gain_momentum.reshape(1, rows))
        keys, ig, nw, nm, ng, ngm = pl.pallas_call(
            store,
            out_shape=shapes,
            in_specs=[vm] * 6,
            out_specs=[hbm] * 6,
            scratch_shapes=[dma((6,))],
        )(*outs)
        return keys, ig, nw, nm, ng.reshape(rows), ngm.reshape(rows)

    in_specs = (
        P(("island", "fsdp"), None),
        P(("island", "fsdp"), None),
        P("fsdp", None),
        P("fsdp"),
        P("fsdp", None),
        P("fsdp"),
    )
    out_specs = (
        P(("island", "fsdp"), None),
        P(("island", "fsdp"), None),
        P("fsdp", None),
        P("fsdp", None),
        P("fsdp"),
        P("fsdp"),
    )
    return jax.shard_map(shards, mesh=mesh, in_specs=in_specs, out_specs=out_specs, check_vma=False)
```

```python
import functools

import jax
import jax.numpy as jnp
from jax import lax
from jax.experimental import pallas as pl
from jax.experimental.pallas import tpu as pltpu
from jax.sharding import PartitionSpec as P

epsilon = 1e-05
inner_rate = 0.5
gain_rate = 0.02
beta_momentum = 0.9
outer_rate = 0.7

MESH = pl.DeviceIdType.MESH
F32, BF16 = jnp.float32, jnp.bfloat16


def kernel(
    n_isl, a, b,
    x_hbm, kg_hbm, w_hbm, g_hbm, m_hbm, gm_hbm,
    keys_ref, ig_ref, nw_ref, nm_ref, ng_ref, ngm_ref,
    x_ref, kg_ref, w_ref, g_ref, m_ref, gm_ref, gw, xs, xr, kr, gs, gr, ge, dx, kacc, load,
    z_s, z_r, y_s, y_r, x_s, x_r, c_s, c_r, t_s, t_r, k_s, k_r, g_s, g_r, e_s, e_r,
):
    nq = 2 * b
    n = a * nq
    tokens, width = x_ref.shape
    rows, feats = w_ref.shape
    scale = width ** (-0.5)
    isl = lax.axis_index("island")
    f = lax.axis_index("fsdp")
    z, q = f // nq, f % nq
    y, core = q // 2, q % 2
    sib = y * 2 + 1 - core
    half = isl % 2
    partner = isl + 1 - 2 * half

    def dev(i, zz, qq):
        return (i, zz * nq + qq)

    def remote(src, dst, ss, rs, to):
        return pltpu.make_async_remote_copy(
            src_ref=src, dst_ref=dst, send_sem=ss, recv_sem=rs, device_id=to, device_id_type=MESH
        )

    zs_ = [lax.rem(z + k, a) for k in range(a)]
    qs_ = [lax.rem(q + k, nq) for k in range(nq)]
    ys_ = [lax.rem(y + k, b) for k in range(b)]
    is_ = [lax.rem(isl + k, n_isl) for k in range(n_isl)]

    loads = [
        pltpu.make_async_copy(src, dst, load.at[i])
        for i, (src, dst) in enumerate(
            ((w_hbm, w_ref), (kg_hbm, kg_ref), (x_hbm, x_ref), (m_hbm, m_ref),
             (g_hbm, g_ref), (gm_hbm, gm_ref))
        )
    ]
    for copy in loads:
        copy.start()
    barrier = pltpu.get_barrier_semaphore()
    for k in range(1, a):
        pl.semaphore_signal(barrier, inc=1, device_id=dev(isl, zs_[k], q), device_id_type=MESH)
    for k in range(1, nq):
        pl.semaphore_signal(barrier, inc=1, device_id=dev(isl, z, qs_[k]), device_id_type=MESH)
    for k in range(1, n_isl):
        pl.semaphore_signal(barrier, inc=1, device_id=dev(is_[k], z, q), device_id_type=MESH)

    loads[4].wait()
    loads[0].wait()
    lanes = min(rows, 128)
    gain_col = jnp.concatenate(
        [
            jnp.broadcast_to(
                g_ref[0:1, j * lanes : (j + 1) * lanes].astype(BF16).astype(F32), (lanes, lanes)
            ).T[:, 0:1]
            for j in range(rows // lanes)
        ],
        axis=0,
    )
    w_b = w_ref[...].astype(BF16).astype(F32)
    gw[z, q] = (w_b * gain_col).astype(BF16).reshape(2, rows // 2, feats)
    pl.semaphore_wait(barrier, a - 1 + nq - 1 + n_isl - 1)

    sends = []

    def go(copy):
        copy.start()
        sends.append(copy)

    def z_copy(k):
        p = gw.at[z, q, half]
        return remote(p, p, z_s.at[k], z_r.at[k], dev(isl, zs_[k], q))

    def z_wait(k):
        p = gw.at[lax.rem(z + a - k, a), q, half]
        remote(p, p, z_s.at[k], z_r.at[k], dev(isl, zs_[k], q)).wait_recv()

    def y_copy(zk, k):
        p = gw.at[lax.rem(z + a - zk, a), q, half]
        return remote(p, p, y_s.at[zk, k], y_r.at[zk, k], dev(isl, z, ys_[k] * 2 + core))

    def y_wait(zk, k):
        p = gw.at[lax.rem(z + a - zk, a), lax.rem(y + b - k, b) * 2 + core, half]
        remote(p, p, y_s.at[zk, k], y_r.at[zk, k], dev(isl, z, q)).wait_recv()

    def piece(zk, k):
        return lax.rem(z + a - zk, a), lax.rem(y + b - k, b) * 2 + core

    def x_copy(zk, k):
        zz, qq = piece(zk, k)
        p = gw.at[zz, qq, half]
        return remote(p, p, x_s.at[zk, k], x_r.at[zk, k], dev(partner, z, q))

    def x_wait(zk, k):
        zz, qq = piece(zk, k)
        p = gw.at[zz, qq, 1 - half]
        remote(p, p, x_s.at[zk, k], x_r.at[zk, k], dev(partner, z, q)).wait_recv()

    def c_copy(zk, k, h):
        zz, qq = piece(zk, k)
        p = gw.at[zz, qq, lax.rem(half + h, 2)]
        return remote(p, p, c_s.at[zk, k, h], c_r.at[zk, k, h], dev(isl, z, sib))

    def c_wait(zk, k, h):
        zz, qq = piece(zk, k)
        p = gw.at[zz, qq + 1 - 2 * core, lax.rem(half + h, 2)]
        remote(p, p, c_s.at[zk, k, h], c_r.at[zk, k, h], dev(isl, z, sib)).wait_recv()

    for k in range(1, a):
        go(z_copy(k))
    loads[1].wait()

    for k in range(1, nq):
        go(remote(kg_ref, kr.at[q], k_s.at[k], k_r.at[k], dev(isl, z, qs_[k])))

    loads[2].wait()
    acc = jnp.zeros((tokens, rows), F32)
    for p in range(n):
        xc = x_ref[:, p * rows : (p + 1) * rows].astype(F32)
        acc = acc + xc * xc
    r = lax.rsqrt(jnp.sum(acc, axis=1, keepdims=True) * (1.0 / width) + epsilon)
    for p in range(n):
        xc = x_ref[:, p * rows : (p + 1) * rows].astype(F32)
        xs[p % nq, p // nq] = (xc * r).astype(BF16)
    near = list(range(1, a)) + [0]
    for j in near:
        for k in range(1, nq):
            go(
                remote(
                    xs.at[qs_[k], zs_[j]], xr.at[q, zs_[j]],
                    t_s.at[j, k], t_r.at[j, k], dev(isl, z, qs_[k]),
                )
            )
    xr[q] = xs[q]
    kr[q] = kg_ref[...]

    for k in range(1, b):
        go(y_copy(0, k))
    for h in range(2):
        go(c_copy(0, 0, h))

    for zk in range(1, a):
        z_wait(zk)
        for k in range(1, b):
            go(y_copy(zk, k))
        go(x_copy(zk, 0))
        go(c_copy(zk, 0, 0))

    for k in range(1, nq):
        src = lax.rem(q + nq - k, nq)
        remote(kg_ref, kr.at[src], k_s.at[k], k_r.at[k], dev(isl, z, q)).wait_recv()

    def partial(j):
        zz = zs_[j]
        for k in range(1, nq):
            src = lax.rem(q + nq - k, nq)
            remote(
                xs.at[q, zz], xr.at[src, zz], t_s.at[j, k], t_r.at[j, k], dev(isl, z, q)
            ).wait_recv()
        return lax.dot_general(
            xr[:, zz].reshape(nq * tokens, rows),
            kr[...].reshape(nq * tokens, feats),
            (((0,), (0,)), ((), ())),
            preferred_element_type=F32,
        )

    for k in range(1, a):
        gs[k] = partial(k).astype(BF16)
        go(remote(gs.at[k], gr.at[k], g_s.at[k], g_r.at[k], dev(isl, zs_[k], q)))
    own = partial(0)

    for zk in range(a):
        for k in range(1, b):
            y_wait(zk, k)
            go(x_copy(zk, k))
            go(c_copy(zk, k, 0))

    for k in range(1, a):
        remote(gs.at[k], gr.at[k], g_s.at[k], g_r.at[k], dev(isl, z, q)).wait_recv()
        own = own + gr[k].astype(F32)
    ge[isl] = own.astype(BF16)
    for k in range(1, n_isl):
        go(remote(ge.at[isl], ge.at[isl], e_s.at[k], e_r.at[k], dev(is_[k], z, q)))

    kacc[...] = jnp.zeros_like(kacc)

    def use(zz, qq):
        p = gw[zz, qq].reshape(rows, feats)
        kacc[...] += jnp.dot(xs[qq, zz], p, preferred_element_type=F32)
        dx[qq, zz] = lax.dot_general(
            kg_ref[...], p, (((1,), (1,)), ((), ())), preferred_element_type=F32
        )

    order = [(zk, k) for k in range(b) for zk in range(a)]
    for zk, k in order:
        if (zk, k) != (0, 0):
            x_wait(zk, k)
            go(c_copy(zk, k, 1))
        use(*piece(zk, k))
    for zk, k in order:
        c_wait(zk, k, 0)
        c_wait(zk, k, 1)
        zz, qq = piece(zk, k)
        use(zz, qq + 1 - 2 * core)

    keys_ref[...] = (kacc[...] * scale).astype(BF16)
    acc = jnp.zeros((tokens, rows), F32)
    for p in range(n):
        xh = x_ref[:, p * rows : (p + 1) * rows].astype(F32) * r
        acc = acc + dx[p % nq, p // nq] * xh
    mean = jnp.sum(acc, axis=1, keepdims=True) * (scale / width)
    for p in range(n):
        cols = slice(p * rows, (p + 1) * rows)
        xh = x_ref[:, cols].astype(F32) * r
        ig_ref[:, cols] = (r * (dx[p % nq, p // nq] * scale - xh * mean)).astype(BF16)

    for k in range(1, n_isl):
        src = lax.rem(isl + n_isl - k, n_isl)
        remote(ge.at[src], ge.at[src], e_s.at[k], e_r.at[k], dev(isl, z, q)).wait_recv()
    total = ge[0].astype(F32)
    for k in range(1, n_isl):
        total = total + ge[k].astype(F32)
    total = total * (scale / n_isl)
    delta = total * gain_col * inner_rate
    w = w_ref[...]
    loads[3].wait()
    loads[5].wait()
    fresh = beta_momentum * m_ref[...] + delta
    nm_ref[...] = fresh
    nw_ref[...] = w - outer_rate * (delta + beta_momentum * fresh)
    gain_sum = jnp.sum(w.astype(BF16).astype(F32) * total, axis=1, keepdims=True) * gain_rate
    for j in range(rows // lanes):
        s = slice(j * lanes, (j + 1) * lanes)
        d = jnp.broadcast_to(gain_sum[s], (lanes, lanes)).T[0:1]
        fresh = beta_momentum * gm_ref[0:1, s] + d
        ngm_ref[0:1, s] = fresh
        ng_ref[0:1, s] = g_ref[0:1, s] - outer_rate * (d + beta_momentum * fresh)

    for copy in sends:
        copy.wait_send()


def store(*refs):
    k = (len(refs) - 1) // 2
    sem = refs[-1]
    copies = [pltpu.make_async_copy(refs[i], refs[k + i], sem.at[i]) for i in range(k)]
    for copy in copies:
        copy.start()
    for copy in copies:
        copy.wait()


def solution(mesh):
    n_isl, n = mesh.shape["island"], mesh.shape["fsdp"]
    b = 1
    while 4 * b * b <= n // 2:
        b *= 2
    a = n // 2 // b
    nq = 2 * b

    def shards(inputs, key_grad, weight, gain, momentum, gain_momentum):
        tokens, width = inputs.shape
        rows, feats = weight.shape
        sd = jax.ShapeDtypeStruct
        dma = pltpu.SemaphoreType.DMA
        vm = pl.BlockSpec(memory_space=pltpu.VMEM)
        hbm = pl.BlockSpec(memory_space=pltpu.HBM)
        shapes = (
            sd((tokens, feats), BF16),
            sd((tokens, width), BF16),
            sd((rows, feats), F32),
            sd((rows, feats), F32),
            sd((1, rows), F32),
            sd((1, rows), F32),
        )
        stay = functools.partial(pltpu.with_memory_space_constraint, memory_space=pltpu.HBM)
        outs = pl.pallas_call(
            functools.partial(kernel, n_isl, a, b),
            out_shape=shapes,
            in_specs=[hbm] * 6,
            out_specs=[vm] * 6,
            scratch_shapes=[
                pltpu.VMEM((tokens, width), BF16),
                pltpu.VMEM((tokens, feats), BF16),
                pltpu.VMEM((rows, feats), F32),
                pltpu.VMEM((1, rows), F32),
                pltpu.VMEM((rows, feats), F32),
                pltpu.VMEM((1, rows), F32),
                pltpu.VMEM((a, nq, 2, rows // 2, feats), BF16),
                pltpu.VMEM((nq, a, tokens, rows), BF16),
                pltpu.VMEM((nq, a, tokens, rows), BF16),
                pltpu.VMEM((nq, tokens, feats), BF16),
                pltpu.VMEM((a, rows, feats), BF16),
                pltpu.VMEM((a, rows, feats), BF16),
                pltpu.VMEM((n_isl, rows, feats), BF16),
                pltpu.VMEM((nq, a, tokens, rows), F32),
                pltpu.VMEM((tokens, feats), F32),
                dma((6,)),
                dma((a,)), dma((a,)),
                dma((a, b)), dma((a, b)),
                dma((a, b)), dma((a, b)),
                dma((a, b, 2)), dma((a, b, 2)),
                dma((a, nq)), dma((a, nq)),
                dma((nq,)), dma((nq,)),
                dma((a,)), dma((a,)),
                dma((n_isl,)), dma((n_isl,)),
            ],
            compiler_params=pltpu.CompilerParams(
                collective_id=0, has_side_effects=True, vmem_limit_bytes=48 << 20
            ),
        )(
            stay(inputs), stay(key_grad), stay(weight), stay(gain.reshape(1, rows)),
            stay(momentum), stay(gain_momentum.reshape(1, rows)),
        )
        keys, ig, nw, nm, ng, ngm = pl.pallas_call(
            store,
            out_shape=shapes,
            in_specs=[pl.BlockSpec(memory_space=pl.ANY)] * 6,
            out_specs=[hbm] * 6,
            scratch_shapes=[dma((6,))],
            compiler_params=pltpu.CompilerParams(vmem_limit_bytes=1 << 20),
        )(*outs)
        return keys, ig, nw, nm, ng.reshape(rows), ngm.reshape(rows)

    in_specs = (
        P(("island", "fsdp"), None),
        P(("island", "fsdp"), None),
        P("fsdp", None),
        P("fsdp"),
        P("fsdp", None),
        P("fsdp"),
    )
    out_specs = (
        P(("island", "fsdp"), None),
        P(("island", "fsdp"), None),
        P("fsdp", None),
        P("fsdp", None),
        P("fsdp"),
        P("fsdp"),
    )
    return jax.shard_map(shards, mesh=mesh, in_specs=in_specs, out_specs=out_specs, check_vma=False)
```

```python
import functools

import jax
import jax.numpy as jnp
from jax import lax
from jax.experimental import pallas as pl
from jax.experimental.pallas import tpu as pltpu
from jax.sharding import PartitionSpec as P

epsilon = 1e-05
inner_rate = 0.5
gain_rate = 0.02
beta_momentum = 0.9
outer_rate = 0.7

MESH = pl.DeviceIdType.MESH
F32, BF16 = jnp.float32, jnp.bfloat16


def kernel(
    n_isl, a, b,
    x_hbm, kg_hbm, w_hbm, g_hbm, m_hbm, gm_hbm,
    keys_ref, ig_ref, nw_ref, nm_ref, ng_ref, ngm_ref,
    x_ref, kg_ref, w_ref, g_ref, m_ref, gm_ref, gw, xs, xr, kr, gs, gr, ge, dx, kacc, load,
    z_s, z_r, y_s, y_r, x_s, x_r, c_s, c_r, t_s, t_r, k_s, k_r, g_s, g_r, e_s, e_r,
):
    nq = 2 * b
    n = a * nq
    tokens, width = x_ref.shape
    rows, feats = w_ref.shape
    scale = width ** (-0.5)
    isl = lax.axis_index("island")
    f = lax.axis_index("fsdp")
    z, q = f // nq, f % nq
    y, core = q // 2, q % 2
    sib = y * 2 + 1 - core
    half = isl % 2
    partner = isl + 1 - 2 * half

    def dev(i, zz, qq):
        return (i, zz * nq + qq)

    def remote(src, dst, ss, rs, to):
        return pltpu.make_async_remote_copy(
            src_ref=src, dst_ref=dst, send_sem=ss, recv_sem=rs, device_id=to, device_id_type=MESH
        )

    zs_ = [lax.rem(z + k, a) for k in range(a)]
    qs_ = [lax.rem(q + k, nq) for k in range(nq)]
    ys_ = [lax.rem(y + k, b) for k in range(b)]
    is_ = [lax.rem(isl + k, n_isl) for k in range(n_isl)]

    loads = [
        pltpu.make_async_copy(src, dst, load.at[i])
        for i, (src, dst) in enumerate(
            ((w_hbm, w_ref), (kg_hbm, kg_ref), (x_hbm, x_ref), (m_hbm, m_ref),
             (g_hbm, g_ref), (gm_hbm, gm_ref))
        )
    ]
    for copy in loads:
        copy.start()
    barrier = pltpu.get_barrier_semaphore()
    for k in range(1, a):
        pl.semaphore_signal(barrier, inc=1, device_id=dev(isl, zs_[k], q), device_id_type=MESH)
    for k in range(1, nq):
        pl.semaphore_signal(barrier, inc=1, device_id=dev(isl, z, qs_[k]), device_id_type=MESH)
    for k in range(1, n_isl):
        pl.semaphore_signal(barrier, inc=1, device_id=dev(is_[k], z, q), device_id_type=MESH)

    loads[4].wait()
    loads[0].wait()
    lanes = min(rows, 128)
    gain_col = jnp.concatenate(
        [
            jnp.broadcast_to(
                g_ref[0:1, j * lanes : (j + 1) * lanes].astype(BF16).astype(F32), (lanes, lanes)
            ).T[:, 0:1]
            for j in range(rows // lanes)
        ],
        axis=0,
    )
    w_b = w_ref[...].astype(BF16).astype(F32)
    gw[z, q] = (w_b * gain_col).astype(BF16).reshape(2, rows // 2, feats)
    pl.semaphore_wait(barrier, a - 1 + nq - 1 + n_isl - 1)

    sends = []

    def go(copy):
        copy.start()
        sends.append(copy)

    def z_copy(k):
        p = gw.at[z, q, half]
        return remote(p, p, z_s.at[k], z_r.at[k], dev(isl, zs_[k], q))

    def z_wait(k):
        p = gw.at[lax.rem(z + a - k, a), q, half]
        remote(p, p, z_s.at[k], z_r.at[k], dev(isl, zs_[k], q)).wait_recv()

    def y_copy(zk, k):
        p = gw.at[lax.rem(z + a - zk, a), q, half]
        return remote(p, p, y_s.at[zk, k], y_r.at[zk, k], dev(isl, z, ys_[k] * 2 + core))

    def y_wait(zk, k):
        p = gw.at[lax.rem(z + a - zk, a), lax.rem(y + b - k, b) * 2 + core, half]
        remote(p, p, y_s.at[zk, k], y_r.at[zk, k], dev(isl, z, q)).wait_recv()

    def piece(zk, k):
        return lax.rem(z + a - zk, a), lax.rem(y + b - k, b) * 2 + core

    def x_copy(zk, k):
        zz, qq = piece(zk, k)
        p = gw.at[zz, qq, half]
        return remote(p, p, x_s.at[zk, k], x_r.at[zk, k], dev(partner, z, q))

    def x_wait(zk, k):
        zz, qq = piece(zk, k)
        p = gw.at[zz, qq, 1 - half]
        remote(p, p, x_s.at[zk, k], x_r.at[zk, k], dev(partner, z, q)).wait_recv()

    def c_copy(zk, k, h):
        zz, qq = piece(zk, k)
        p = gw.at[zz, qq, lax.rem(half + h, 2)]
        return remote(p, p, c_s.at[zk, k, h], c_r.at[zk, k, h], dev(isl, z, sib))

    def c_wait(zk, k, h):
        zz, qq = piece(zk, k)
        p = gw.at[zz, qq + 1 - 2 * core, lax.rem(half + h, 2)]
        remote(p, p, c_s.at[zk, k, h], c_r.at[zk, k, h], dev(isl, z, sib)).wait_recv()

    for k in range(1, a):
        go(z_copy(k))
    loads[1].wait()

    for k in range(1, nq):
        go(remote(kg_ref, kr.at[q], k_s.at[k], k_r.at[k], dev(isl, z, qs_[k])))

    for k in range(1, b):
        go(y_copy(0, k))
    for h in range(2):
        go(c_copy(0, 0, h))

    loads[2].wait()
    acc = jnp.zeros((tokens, rows), F32)
    for p in range(n):
        xc = x_ref[:, p * rows : (p + 1) * rows].astype(F32)
        acc = acc + xc * xc
    r = lax.rsqrt(jnp.sum(acc, axis=1, keepdims=True) * (1.0 / width) + epsilon)
    for p in range(n):
        xc = x_ref[:, p * rows : (p + 1) * rows].astype(F32)
        xs[p % nq, p // nq] = (xc * r).astype(BF16)
    near = list(range(1, a)) + [0]
    for j in near:
        for k in range(1, nq):
            go(
                remote(
                    xs.at[qs_[k], zs_[j]], xr.at[q, zs_[j]],
                    t_s.at[j, k], t_r.at[j, k], dev(isl, z, qs_[k]),
                )
            )
    xr[q] = xs[q]
    kr[q] = kg_ref[...]

    for zk in range(1, a):
        z_wait(zk)
        for k in range(1, b):
            go(y_copy(zk, k))
        go(x_copy(zk, 0))
        go(c_copy(zk, 0, 0))

    for k in range(1, b):
        y_wait(0, k)
        go(x_copy(0, k))
        go(c_copy(0, k, 0))

    for k in range(1, nq):
        src = lax.rem(q + nq - k, nq)
        remote(kg_ref, kr.at[src], k_s.at[k], k_r.at[k], dev(isl, z, q)).wait_recv()

    def partial(j):
        zz = zs_[j]
        for k in range(1, nq):
            src = lax.rem(q + nq - k, nq)
            remote(
                xs.at[q, zz], xr.at[src, zz], t_s.at[j, k], t_r.at[j, k], dev(isl, z, q)
            ).wait_recv()
        return lax.dot_general(
            xr[:, zz].reshape(nq * tokens, rows),
            kr[...].reshape(nq * tokens, feats),
            (((0,), (0,)), ((), ())),
            preferred_element_type=F32,
        )

    for k in range(1, a):
        gs[k] = partial(k).astype(BF16)
        go(remote(gs.at[k], gr.at[k], g_s.at[k], g_r.at[k], dev(isl, zs_[k], q)))
    own = partial(0)

    for zk in range(1, a):
        for k in range(1, b):
            y_wait(zk, k)
            go(x_copy(zk, k))
            go(c_copy(zk, k, 0))

    for k in range(1, a):
        remote(gs.at[k], gr.at[k], g_s.at[k], g_r.at[k], dev(isl, z, q)).wait_recv()
        own = own + gr[k].astype(F32)
    ge[isl] = own.astype(BF16)
    for k in range(1, n_isl):
        go(remote(ge.at[isl], ge.at[isl], e_s.at[k], e_r.at[k], dev(is_[k], z, q)))

    kacc[...] = jnp.zeros_like(kacc)

    def use(zz, qq):
        p = gw[zz, qq].reshape(rows, feats)
        kacc[...] += jnp.dot(xs[qq, zz], p, preferred_element_type=F32)
        dx[qq, zz] = lax.dot_general(
            kg_ref[...], p, (((1,), (1,)), ((), ())), preferred_element_type=F32
        )

    order = [(zk, k) for k in range(b) for zk in range(a)]
    for zk, k in order:
        if (zk, k) != (0, 0):
            x_wait(zk, k)
            go(c_copy(zk, k, 1))
        use(*piece(zk, k))
    for zk, k in order:
        c_wait(zk, k, 0)
        c_wait(zk, k, 1)
        zz, qq = piece(zk, k)
        use(zz, qq + 1 - 2 * core)

    keys_ref[...] = (kacc[...] * scale).astype(BF16)
    acc = jnp.zeros((tokens, rows), F32)
    for p in range(n):
        xh = x_ref[:, p * rows : (p + 1) * rows].astype(F32) * r
        acc = acc + dx[p % nq, p // nq] * xh
    mean = jnp.sum(acc, axis=1, keepdims=True) * (scale / width)
    for p in range(n):
        cols = slice(p * rows, (p + 1) * rows)
        xh = x_ref[:, cols].astype(F32) * r
        ig_ref[:, cols] = (r * (dx[p % nq, p // nq] * scale - xh * mean)).astype(BF16)

    for k in range(1, n_isl):
        src = lax.rem(isl + n_isl - k, n_isl)
        remote(ge.at[src], ge.at[src], e_s.at[k], e_r.at[k], dev(isl, z, q)).wait_recv()
    total = ge[0].astype(F32)
    for k in range(1, n_isl):
        total = total + ge[k].astype(F32)
    total = total * (scale / n_isl)
    delta = total * gain_col * inner_rate
    w = w_ref[...]
    loads[3].wait()
    loads[5].wait()
    fresh = beta_momentum * m_ref[...] + delta
    nm_ref[...] = fresh
    nw_ref[...] = w - outer_rate * (delta + beta_momentum * fresh)
    gain_sum = jnp.sum(w.astype(BF16).astype(F32) * total, axis=1, keepdims=True) * gain_rate
    for j in range(rows // lanes):
        s = slice(j * lanes, (j + 1) * lanes)
        d = jnp.broadcast_to(gain_sum[s], (lanes, lanes)).T[0:1]
        fresh = beta_momentum * gm_ref[0:1, s] + d
        ngm_ref[0:1, s] = fresh
        ng_ref[0:1, s] = g_ref[0:1, s] - outer_rate * (d + beta_momentum * fresh)

    for copy in sends:
        copy.wait_send()


def store(*refs):
    k = (len(refs) - 1) // 2
    sem = refs[-1]
    copies = [pltpu.make_async_copy(refs[i], refs[k + i], sem.at[i]) for i in range(k)]
    for copy in copies:
        copy.start()
    for copy in copies:
        copy.wait()


def solution(mesh):
    n_isl, n = mesh.shape["island"], mesh.shape["fsdp"]
    b = 1
    while 4 * b * b <= n // 2:
        b *= 2
    a = n // 2 // b
    nq = 2 * b

    def shards(inputs, key_grad, weight, gain, momentum, gain_momentum):
        tokens, width = inputs.shape
        rows, feats = weight.shape
        sd = jax.ShapeDtypeStruct
        dma = pltpu.SemaphoreType.DMA
        vm = pl.BlockSpec(memory_space=pltpu.VMEM)
        hbm = pl.BlockSpec(memory_space=pltpu.HBM)
        shapes = (
            sd((tokens, feats), BF16),
            sd((tokens, width), BF16),
            sd((rows, feats), F32),
            sd((rows, feats), F32),
            sd((1, rows), F32),
            sd((1, rows), F32),
        )
        stay = functools.partial(pltpu.with_memory_space_constraint, memory_space=pltpu.HBM)
        outs = pl.pallas_call(
            functools.partial(kernel, n_isl, a, b),
            out_shape=shapes,
            in_specs=[hbm] * 6,
            out_specs=[vm] * 6,
            scratch_shapes=[
                pltpu.VMEM((tokens, width), BF16),
                pltpu.VMEM((tokens, feats), BF16),
                pltpu.VMEM((rows, feats), F32),
                pltpu.VMEM((1, rows), F32),
                pltpu.VMEM((rows, feats), F32),
                pltpu.VMEM((1, rows), F32),
                pltpu.VMEM((a, nq, 2, rows // 2, feats), BF16),
                pltpu.VMEM((nq, a, tokens, rows), BF16),
                pltpu.VMEM((nq, a, tokens, rows), BF16),
                pltpu.VMEM((nq, tokens, feats), BF16),
                pltpu.VMEM((a, rows, feats), BF16),
                pltpu.VMEM((a, rows, feats), BF16),
                pltpu.VMEM((n_isl, rows, feats), BF16),
                pltpu.VMEM((nq, a, tokens, rows), F32),
                pltpu.VMEM((tokens, feats), F32),
                dma((6,)),
                dma((a,)), dma((a,)),
                dma((a, b)), dma((a, b)),
                dma((a, b)), dma((a, b)),
                dma((a, b, 2)), dma((a, b, 2)),
                dma((a, nq)), dma((a, nq)),
                dma((nq,)), dma((nq,)),
                dma((a,)), dma((a,)),
                dma((n_isl,)), dma((n_isl,)),
            ],
            compiler_params=pltpu.CompilerParams(
                collective_id=0, has_side_effects=True, vmem_limit_bytes=48 << 20
            ),
        )(
            stay(inputs), stay(key_grad), stay(weight), stay(gain.reshape(1, rows)),
            stay(momentum), stay(gain_momentum.reshape(1, rows)),
        )
        keys, ig, nw, nm, ng, ngm = pl.pallas_call(
            store,
            out_shape=shapes,
            in_specs=[pl.BlockSpec(memory_space=pl.ANY)] * 6,
            out_specs=[hbm] * 6,
            scratch_shapes=[dma((6,))],
            compiler_params=pltpu.CompilerParams(vmem_limit_bytes=1 << 20),
        )(*outs)
        return keys, ig, nw, nm, ng.reshape(rows), ngm.reshape(rows)

    in_specs = (
        P(("island", "fsdp"), None),
        P(("island", "fsdp"), None),
        P("fsdp", None),
        P("fsdp"),
        P("fsdp", None),
        P("fsdp"),
    )
    out_specs = (
        P(("island", "fsdp"), None),
        P(("island", "fsdp"), None),
        P("fsdp", None),
        P("fsdp", None),
        P("fsdp"),
        P("fsdp"),
    )
    return jax.shard_map(shards, mesh=mesh, in_specs=in_specs, out_specs=out_specs, check_vma=False)
```
